32 devices in a mesh: swath: 2 (over x), rng: 16 (over z, y, core).
Axes of the slice: x: 2, y: 2, z: 4, core: 2. Of those that a mesh axis runs over, the one named last changes fastest.
Arguments:
- echoes: float32 [2, 512, 32768], P(None, ('swath', 'rng')), parts along dimension 1, may hold values from -6 to 6
- doppler_filter: float32 [2, 32768], replicated, may hold values from -5 to 5
- migration_shift: int32 [32768], replicated, may hold values from 0 to 9, as said below
- kernel_index: int32 [32768], replicated, may hold values from 0 to 15
- kernel_taps: float32 [16, 16], replicated, may hold values from -1.5 to 1.5
Outputs:
- image: float32 [2, 512, 32768], P(None, ('swath', 'rng')), parts along dimension 1
The draws below stay inside these ranges and needn't reach their ends.
There are 2 independent parts, one for each index of `swath`. The reference program is written for one: setup_inputs(seed, part) draws one part's arguments, and reference() takes and returns one part's arrays. A program takes and returns all parts, laid end to end along the dimension named above; an argument that names none is the same for every part. Nothing has to cross between parts.
Inputs may be any that keep to these rules, and one draw needn't show every extreme that they name: `migration_shift`: both 0 and 9 occur.
All inputs are finite; a program needn't handle non-finite values.
Results may differ from the reference program's by a relative error of at most 0.0041.
Values may be sent and summed in bfloat16 or wider, within the bound.
A program may use at most 64 MiB of HBM per device.

```python
import math
import jax
import jax.numpy as jnp
from jax import lax

PULSES = 32768
RANGE = 256
TAPS = 16
NKER = 16
SMAX = 9


def draw_migration_shift(key, part):
    key_values, key_top, key_gap = jax.random.split(key, 3)
    values = jax.random.randint(key_values, (PULSES,), 0, SMAX + 1)
    where_top = jax.random.randint(key_top, (), 0, PULSES)
    distance = jax.random.randint(key_gap, (), 1, PULSES)
    where_zero = (where_top + distance) % PULSES
    positions = jnp.arange(PULSES, dtype=jnp.int32)
    values = jnp.where(positions == where_top, SMAX, values)
    return jnp.where(positions == where_zero, 0, values).astype(jnp.int32)


def place_ends(values, rng, low, top_value):
    shape = values.shape
    index_at = [jax.random.randint(jax.random.fold_in(rng, axis), (), 0, shape[axis]) for axis in range(len(shape))]
    values = values.at[tuple(index_at)].set(low)
    longest = shape.index(max(shape))
    index_at[longest] = (index_at[longest] + 1) % shape[longest]
    return values.at[tuple(index_at)].set(top_value)


def block_scale(stream_key, dims, shards, low, top_value):
    def one(axis_at, shards_of):
        draws = jax.random.uniform(jax.random.fold_in(jax.random.fold_in(stream_key, 6), axis_at), (shards_of,), jnp.float32, low / len(shards), top_value / len(shards))
        return jnp.repeat(jnp.exp(draws), dims[axis_at] // shards_of).reshape((-1,) + (1,) * (len(dims) - axis_at - 1))

    level = one(*shards[0])
    for cut in shards[1:]:
        level = level * one(*cut)
    return level


def normal_values(key, dims, deviation, limit, cuts=(), kind=jnp.bfloat16):
    values = jax.random.normal(key, dims, jnp.float32) * deviation
    if len(cuts) > 0:
        values = block_scale(key, dims, cuts, -0.22, 0.18) * values
    return jnp.clip(values, min=-limit, max=limit).astype(kind)


def setup_inputs(seed: int = 0, part: int = 0) -> dict:
    seeds = jax.random.split(jax.random.key(seed), 6)
    own_keys = jax.random.split(jax.random.fold_in(seeds[5], part), 6)
    echoes = normal_values(own_keys[0], (2, RANGE, PULSES), 1.0, 6.0, ((1, 16),), jnp.float32)
    doppler_filter = normal_values(seeds[1], (2, PULSES), 0.7, 5.0, (), jnp.float32)
    migration_shift = draw_migration_shift(jax.random.fold_in(seeds[5], 71), part)
    kernel_index = place_ends(jax.random.randint(seeds[3], (PULSES,), 0, NKER), jax.random.fold_in(seeds[3], 1), 0, NKER - 1).astype(jnp.int32)
    kernel_taps = normal_values(seeds[4], (NKER, TAPS), TAPS ** -0.5, 1.5, (), jnp.float32)
    return dict(echoes=echoes, doppler_filter=doppler_filter, migration_shift=migration_shift, kernel_index=kernel_index, kernel_taps=kernel_taps)


def reference(echoes, doppler_filter, migration_shift, kernel_index, kernel_taps):
    norm_scale = 1.0 / math.sqrt(PULSES)
    samples = lax.complex(echoes[0], echoes[1])
    spectrum = jnp.fft.fft(samples, axis=1) * norm_scale
    response = lax.complex(doppler_filter[0], -doppler_filter[1])
    weighted = spectrum * response[None, :]
    filtered = jnp.stack([jnp.real(weighted), jnp.imag(weighted)]).astype(jnp.bfloat16)
    coefficients = kernel_taps[kernel_index]
    tap_numbers = jnp.arange(TAPS, dtype=jnp.int32)
    low_margin = SMAX + TAPS // 2 - 1
    padded = jnp.pad(filtered, ((0, 0), (low_margin, TAPS // 2), (0, 0)))
    running = jnp.zeros((2, RANGE, PULSES), jnp.float32)
    for offset_slot in range(TAPS + SMAX):
        chosen = (tap_numbers[None, :] == (offset_slot - migration_shift)[:, None]).astype(jnp.float32)
        column_weight = lax.optimization_barrier(jnp.sum(coefficients * chosen, axis=1))
        first_row = low_margin + TAPS // 2 - offset_slot
        segment = padded[:, first_row:first_row + RANGE, :].astype(jnp.float32)
        running = running + column_weight[None, None, :] * segment
    migrated = running.astype(jnp.bfloat16)
    restored = lax.complex(migrated[0].astype(jnp.float32), migrated[1].astype(jnp.float32))
    image_parts = jnp.fft.ifft(restored, axis=1) / norm_scale
    return jnp.stack([jnp.real(image_parts), jnp.imag(image_parts)]).astype(jnp.float32)
```

```python
import functools
import math

import jax
import jax.numpy as jnp
import numpy as np
from jax import lax
from jax.experimental import pallas as pl
from jax.experimental.pallas import tpu as pltpu
from jax.sharding import PartitionSpec as P

F2 = 256
SMAX = 9
GROUP = 8
CHUNK = 16

f32 = jnp.float32
bf16 = jnp.bfloat16


def dft(length):
    numbers = np.arange(length)
    angles = (numbers[:, None] * numbers[None, :] % length) * (2.0 * math.pi / length)
    return np.cos(angles), np.sin(angles)


def split(table):
    table = table.astype(np.float32)
    high = table.astype(bf16)
    return high, (table - high.astype(np.float32)).astype(bf16)


def twiddles(outer, inner):
    angles = (np.arange(outer)[:, None] * np.arange(inner)[None, :]) * (
        2.0 * math.pi / (outer * inner)
    )
    return np.stack([np.cos(angles), np.sin(angles)]).astype(np.float32)


def dot(a, b):
    return jnp.dot(a, b, preferred_element_type=f32)


def halves(value):
    high = value.astype(bf16)
    return high, (value - high.astype(f32)).astype(bf16)


def forward_kernel(outer, inner, x_ref, w1h_ref, w1l_ref, w2h_ref, w2l_ref, t_ref, h_ref, o_ref, rh_ref, rl_ref):
    lanes = 128
    parts = inner // lanes
    stride = GROUP * parts
    w1h = w1h_ref[...]
    w1l = w1l_ref[...]
    for r in range(GROUP):
        columns = []
        for c in range(2):
            columns.append(
                jnp.concatenate(
                    [
                        x_ref[c, 0, pl.ds(h * GROUP + r, outer, stride=stride), :]
                        for h in range(parts)
                    ],
                    axis=1,
                )
            )
        xh, xl = halves(jnp.concatenate(columns, axis=0))
        s = dot(w1h, xh) + dot(w1h, xl) + dot(w1l, xh)
        re, im = s[:outer], s[outer:]
        tc, ts = t_ref[0], t_ref[1]
        rows = pl.ds(r * outer, outer)
        a, b = halves(re * tc + im * ts)
        rh_ref[rows, :inner] = a
        rl_ref[rows, :inner] = b
        a, b = halves(im * tc - re * ts)
        rh_ref[rows, inner:] = a
        rl_ref[rows, inner:] = b
    per = 2
    for g in range(GROUP // per):
        rows = pl.ds(g * per * outer, per * outer)
        rh = rh_ref[rows, :]
        z = dot(rh, w2h_ref[...]) + dot(rh, w2l_ref[...]) + dot(rl_ref[rows, :], w2h_ref[...])
        for j in range(per):
            re = z[j * outer : (j + 1) * outer, :inner]
            im = z[j * outer : (j + 1) * outer, inner:]
            hr, hi = h_ref[0], h_ref[1]
            o_ref[0, 0, g * per + j] = (re * hr + im * hi).astype(bf16)
            o_ref[0, 1, g * per + j] = (im * hr - re * hi).astype(bf16)


def inverse_kernel(outer, inner, rows, taps, chunks, own_ref, prev_ref, next_ref, s_ref, k_ref, tab_ref, t_ref, v2_ref, v1_ref, o_ref, m_ref, y_ref):
    lanes = 128
    parts = inner // lanes
    stride = GROUP * parts
    step = pl.program_id(0)
    low = taps // 2 - 1

    @pl.when(step < chunks)
    def _():
        for sub in range(CHUNK // 8):
            for part in range(parts):
                a = slice(sub * 8, sub * 8 + 8)
                b = slice(part * lanes, part * lanes + lanes)
                offset = SMAX - s_ref[a, b]
                which = k_ref[a, b]
                bits = [(offset & bit) != 0 for bit in (8, 4, 2, 1)]
                weights = [
                    jnp.take_along_axis(tab_ref[k], which, axis=1, mode="promise_in_bounds")
                    for k in range(taps)
                ]
                for c in range(2):
                    line = [prev_ref[g, c, i, a, b] for g in range(rows // GROUP) for i in range(GROUP)]
                    line += [own_ref[g, c, i, a, b] for g in range(rows // GROUP) for i in range(GROUP)]
                    line += [next_ref[0, c, i, a, b] for i in range(GROUP)]
                    line = [v.astype(f32) for v in line]
                    need = rows + taps - 1
                    for n, bit in enumerate((8, 4, 2, 1)):
                        keep = need + (bit - 1)
                        line = [
                            jnp.where(bits[n], line[j + bit], line[j]) if j + bit < len(line) else line[j]
                            for j in range(keep)
                        ]
                    for i in range(rows):
                        total = weights[0] * line[i + taps - 1]
                        for k in range(1, taps):
                            total = total + weights[k] * line[i + taps - 1 - k]
                        m_ref[i, a, c * inner + part * lanes : c * inner + part * lanes + lanes] = total
        flat = m_ref[...].reshape(rows * CHUNK, 2 * inner).astype(bf16)
        z = dot(flat, v2_ref[...]).reshape(rows, CHUNK, 2 * inner)
        re, im = z[:, :, :inner], z[:, :, inner:]
        tc, ts = t_ref[0][None], t_ref[1][None]
        first = pl.multiple_of(step * CHUNK, CHUNK)
        y_ref[:, 0, pl.ds(first, CHUNK), :] = (re * tc - im * ts).astype(bf16)
        y_ref[:, 1, pl.ds(first, CHUNK), :] = (re * ts + im * tc).astype(bf16)

    @pl.when(step >= chunks)
    def _():
        base = (step - chunks) * GROUP
        scale = 1.0 / math.sqrt(outer * inner)
        for r in range(GROUP):
            z = dot(v1_ref[...], y_ref[base + r].reshape(2 * outer, inner)) * scale
            for c in range(2):
                for h in range(parts):
                    o_ref[c, 0, pl.ds(h * GROUP + r, outer, stride=stride), :] = z[
                        c * outer : (c + 1) * outer, h * lanes : (h + 1) * lanes
                    ]


def per_device(echoes, doppler_filter, migration_shift, kernel_index, kernel_taps):
    rows = echoes.shape[1]
    pulses = echoes.shape[2]
    inner = F2
    outer = pulses // inner
    taps = kernel_taps.shape[1]
    groups = rows // GROUP
    tiles = pulses // 128
    count = lax.axis_size("rng")
    whole = lambda *shape: pl.BlockSpec(shape, lambda i: (0,) * len(shape))

    def order(table):
        return jnp.swapaxes(table.reshape(table.shape[:-1] + (inner, outer)), -1, -2)

    oc, osn = dft(outer)
    ic, isn = dft(inner)
    w1h, w1l = split(np.block([[oc, osn], [-osn, oc]]))
    w2h, w2l = split(np.block([[ic, -isn], [isn, ic]]))
    v2 = split(np.block([[ic, isn], [-isn, ic]]))[0]
    v1 = split(np.block([[oc, -osn], [osn, oc]]))[0]
    twist = twiddles(outer, inner)
    response = order(doppler_filter * (1.0 / math.sqrt(pulses)))
    signal = (
        echoes.reshape(2, groups, GROUP, tiles, 128)
        .transpose(0, 1, 3, 2, 4)
        .reshape(2, groups, tiles * GROUP, 128)
    )
    filtered = pl.pallas_call(
        functools.partial(forward_kernel, outer, inner),
        grid=(groups,),
        in_specs=[
            pl.BlockSpec((2, 1, tiles * GROUP, 128), lambda i: (0, i, 0, 0)),
            whole(*w1h.shape),
            whole(*w1h.shape),
            whole(*w2h.shape),
            whole(*w2h.shape),
            whole(*twist.shape),
            whole(*twist.shape),
        ],
        out_specs=pl.BlockSpec((1, 2, GROUP, outer, inner), lambda i: (i, 0, 0, 0, 0)),
        out_shape=jax.ShapeDtypeStruct((groups, 2, GROUP, outer, inner), bf16),
        scratch_shapes=[pltpu.VMEM((GROUP * outer, 2 * inner), bf16)] * 2,
        name="forward",
    )(signal, jnp.asarray(w1h), jnp.asarray(w1l), jnp.asarray(w2h), jnp.asarray(w2l), jnp.asarray(twist), response)
    before = lax.ppermute(filtered, "rng", [(i, i + 1) for i in range(count - 1)])
    after = lax.ppermute(filtered[:1], "rng", [(i + 1, i) for i in range(count - 1)])
    table = jnp.broadcast_to(
        jnp.tile(kernel_taps.T, (1, 128 // kernel_taps.shape[0]))[:, None, :], (taps, 8, 128)
    )
    chunks = outer // CHUNK
    last = chunks - 1
    at = lambda i: jnp.minimum(i, last)
    image = pl.pallas_call(
        functools.partial(inverse_kernel, outer, inner, rows, taps, chunks),
        grid=(chunks + groups,),
        in_specs=[
            pl.BlockSpec((groups, 2, GROUP, CHUNK, inner), lambda i: (0, 0, 0, at(i), 0)),
            pl.BlockSpec((groups, 2, GROUP, CHUNK, inner), lambda i: (0, 0, 0, at(i), 0)),
            pl.BlockSpec((1, 2, GROUP, CHUNK, inner), lambda i: (0, 0, 0, at(i), 0)),
            pl.BlockSpec((CHUNK, inner), lambda i: (at(i), 0)),
            pl.BlockSpec((CHUNK, inner), lambda i: (at(i), 0)),
            whole(taps, 8, 128),
            pl.BlockSpec((2, CHUNK, inner), lambda i: (0, at(i), 0)),
            whole(*v2.shape),
            whole(*v1.shape),
        ],
        out_specs=pl.BlockSpec(
            (2, 1, tiles * GROUP, 128), lambda i: (0, jnp.maximum(i - chunks, 0), 0, 0)
        ),
        out_shape=jax.ShapeDtypeStruct((2, groups, tiles * GROUP, 128), f32),
        scratch_shapes=[
            pltpu.VMEM((rows, CHUNK, 2 * inner), f32),
            pltpu.VMEM((rows, 2, outer, inner), bf16),
        ],
        name="inverse",
    )(filtered, before, after, order(migration_shift), order(kernel_index), table, jnp.asarray(twist), jnp.asarray(v2), jnp.asarray(v1))
    return (
        image.reshape(2, groups, tiles, GROUP, 128)
        .transpose(0, 1, 3, 2, 4)
        .reshape(2, rows, pulses)
    )


def solution(mesh):
    return jax.shard_map(
        per_device,
        mesh=mesh,
        in_specs=(P(None, ("swath", "rng"), None), P(), P(), P(), P()),
        out_specs=P(None, ("swath", "rng"), None),
        check_vma=False,
    )
```

```python
import functools
import math

import jax
import jax.numpy as jnp
import numpy as np
from jax import lax
from jax.experimental import pallas as pl
from jax.experimental.pallas import tpu as pltpu
from jax.sharding import PartitionSpec as P

F2 = 256
SMAX = 9
GROUP = 8
CHUNK = 16

f32 = jnp.float32
bf16 = jnp.bfloat16


def dft(length):
    numbers = np.arange(length)
    angles = (numbers[:, None] * numbers[None, :] % length) * (2.0 * math.pi / length)
    return np.cos(angles), np.sin(angles)


def split(table):
    table = table.astype(np.float32)
    high = table.astype(bf16)
    return high, (table - high.astype(np.float32)).astype(bf16)


def twiddles(outer, inner):
    angles = (np.arange(outer)[:, None] * np.arange(inner)[None, :]) * (
        2.0 * math.pi / (outer * inner)
    )
    return np.stack([np.cos(angles), np.sin(angles)]).astype(np.float32)


def dot(a, b):
    return jnp.dot(a, b, preferred_element_type=f32)


def halves(value):
    high = value.astype(bf16)
    return high, (value - high.astype(f32)).astype(bf16)


def forward_kernel(outer, inner, x_ref, w1h_ref, w1l_ref, w2h_ref, w2l_ref, t_ref, h_ref, o_ref, rh_ref, rl_ref):
    lanes = 128
    parts = inner // lanes
    stride = GROUP * parts
    w1h = w1h_ref[...]
    w1l = w1l_ref[...]
    for r in range(GROUP):
        columns = []
        for c in range(2):
            columns.append(
                jnp.concatenate(
                    [
                        x_ref[c, 0, pl.ds(h * GROUP + r, outer, stride=stride), :]
                        for h in range(parts)
                    ],
                    axis=1,
                )
            )
        xh, xl = halves(jnp.concatenate(columns, axis=0))
        s = dot(w1h, xh) + dot(w1h, xl) + dot(w1l, xh)
        re, im = s[:outer], s[outer:]
        tc, ts = t_ref[0], t_ref[1]
        rows = pl.ds(r * outer, outer)
        a, b = halves(re * tc + im * ts)
        rh_ref[rows, :inner] = a
        rl_ref[rows, :inner] = b
        a, b = halves(im * tc - re * ts)
        rh_ref[rows, inner:] = a
        rl_ref[rows, inner:] = b
    per = 2
    for g in range(GROUP // per):
        rows = pl.ds(g * per * outer, per * outer)
        rh = rh_ref[rows, :]
        z = dot(rh, w2h_ref[...]) + dot(rh, w2l_ref[...]) + dot(rl_ref[rows, :], w2h_ref[...])
        for j in range(per):
            re = z[j * outer : (j + 1) * outer, :inner]
            im = z[j * outer : (j + 1) * outer, inner:]
            hr, hi = h_ref[0], h_ref[1]
            o_ref[0, 0, g * per + j] = (re * hr + im * hi).astype(bf16)
            o_ref[0, 1, g * per + j] = (im * hr - re * hi).astype(bf16)


def exchange_kernel(count, own, s_ref, prev, nxt, mid, low, head, mix, ssem, rsem, lsem):
    me = lax.axis_index("rng")
    role = me % 4
    first = me < 4
    final = me >= count - 4
    half = own.shape[3] // 2
    early, late = range(4), range(4, 8)

    def at(ref, p):
        group = (1 - p // 4) if ref.shape[0] == 2 else 0
        return ref.at[group, (p // 2) % 2, :, pl.ds((p % 2) * half, half), :]

    def copy(kind, p, src, dst, target):
        return pltpu.make_async_remote_copy(
            src_ref=at(src, p),
            dst_ref=at(dst, p),
            send_sem=ssem.at[kind, p],
            recv_sem=rsem.at[kind, p],
            device_id={"rng": target},
            device_id_type=pl.DeviceIdType.MESH,
        )

    def got(kind, p, dst):
        copy(kind, p, dst, dst, (me + 1) % count).wait_recv()

    def merge(p, high, lower):
        rows = pl.ds((p % 2) * half, half)
        limit = SMAX - s_ref[rows, :]
        for j in range(GROUP):
            where = (0, (p // 2) % 2, j, rows)
            mix[where] = jnp.where(
                limit <= j, high[where].astype(f32), lower[where].astype(f32)
            ).astype(bf16)

    def local(src, dst, slot):
        return pltpu.make_async_copy(src, dst, lsem.at[slot])

    @pl.when(role == 0)
    def _():
        sends = [copy(0, p, own, prev, me + 1) for p in range(8)]
        for s in sends:
            s.start()

        @pl.when(first)
        def _():
            low[...] = jnp.zeros_like(low)
            fills = [local(low.at[0], prev.at[g], g) for g in range(2)]
            for f in fills:
                f.start()
            for f in fills:
                f.wait()

        @pl.when(jnp.logical_not(first))
        def _():
            back = [copy(1, p, own, low, me - 3) for p in late]
            for s in back:
                s.start()
            for p in range(8):
                got(3, p, prev)
            for s in back:
                s.wait_send()

        for p in late:
            got(4, p, nxt)
        for s in sends:
            s.wait_send()

    @pl.when(role == 1)
    def _():
        sends = [copy(2, p, own, prev, me + 1) for p in early]
        sends += [copy(2, p, mix, prev, me + 1) for p in late]
        back = [copy(4, p, own, nxt, me - 1) for p in late]
        for p in early:
            sends[p].start()
        for s in back:
            s.start()
        fetch = local(own.at[0], head.at[0], 0)
        fetch.start()
        fetch.wait()

        @pl.when(final)
        def _():
            low[...] = jnp.zeros_like(low)

        def relay(p):
            got(2, p, mid)

            @pl.when(jnp.logical_not(final))
            def _():
                copy(3, p, mid, prev, me + 3).start()

        for p in early:

            @pl.when(jnp.logical_not(final))
            def _():
                got(1, p + 4, low)

            merge(p + 4, head, low)
            sends[p + 4].start()
            relay(p)
        for p in late:
            relay(p)
        out = local(mid.at[0], nxt.at[0], 1)
        out.start()
        for p in range(8):
            got(0, p, prev)
        out.wait()
        for s in sends + back:
            s.wait_send()

        @pl.when(jnp.logical_not(final))
        def _():
            for p in range(8):
                copy(3, p, mid, prev, me + 3).wait_send()

    @pl.when(role == 2)
    def _():
        fetch = local(own.at[0], head.at[0], 0)
        fetch.start()
        sends = [copy(0, p, own, prev, me + 1) for p in range(8)]
        for s in sends:
            s.start()
        over = [copy(2, p, mid, mid, me - 1) for p in early]
        over += [copy(2, p, mix, mid, me - 1) for p in late]
        for p in early:
            got(0, p, mid)
            over[p].start()
        fetch.wait()
        for p in late:
            got(0, p, mid)
            merge(p, mid, head)
            over[p].start()
        out = local(mid.at[0], nxt.at[0], 1)
        out.start()
        pass_on = [copy(3, p, prev, nxt, me + 1) for p in late]
        for p in early:
            got(2, p, prev)
        for p in late:
            got(2, p, prev)
            pass_on[p - 4].start()
        out.wait()
        for s in sends + over + pass_on:
            s.wait_send()

    @pl.when(role == 3)
    def _():
        sends = [copy(0, p, own, mid, me - 1) for p in range(8)]
        for s in sends:
            s.start()
        for p in range(8):
            got(0, p, prev)
        for p in late:
            got(3, p, nxt)
        for s in sends:
            s.wait_send()


def exchange(filtered, shift, count):
    if count % 4 or filtered.shape[0] != 2 or filtered.shape[2] != SMAX - 1:
        before = lax.ppermute(filtered, "rng", [(i, i + 1) for i in range(count - 1)])
        after = lax.ppermute(filtered[:1], "rng", [(i + 1, i) for i in range(count - 1)])
        return before, after
    short = (1,) + filtered.shape[1:]
    anywhere = pl.BlockSpec(memory_space=pl.ANY)
    return pl.pallas_call(
        functools.partial(exchange_kernel, count),
        in_specs=[anywhere, pl.BlockSpec(memory_space=pltpu.VMEM)],
        out_specs=[anywhere, anywhere],
        out_shape=[
            jax.ShapeDtypeStruct(filtered.shape, bf16),
            jax.ShapeDtypeStruct(short, bf16),
        ],
        scratch_shapes=[
            pltpu.VMEM(filtered.shape, bf16),
            pltpu.VMEM(short, bf16),
            pltpu.VMEM(short, bf16),
            pltpu.VMEM(short, bf16),
            pltpu.SemaphoreType.DMA((5, 8)),
            pltpu.SemaphoreType.DMA((5, 8)),
            pltpu.SemaphoreType.DMA((2,)),
        ],
        compiler_params=pltpu.CompilerParams(has_side_effects=True),
        name="exchange",
    )(filtered, shift)


def inverse_kernel(outer, inner, rows, taps, chunks, own_ref, prev_ref, next_ref, s_ref, k_ref, tab_ref, t_ref, v2_ref, v1_ref, o_ref, m_ref, y_ref):
    lanes = 128
    parts = inner // lanes
    stride = GROUP * parts
    step = pl.program_id(0)
    low = taps // 2 - 1

    @pl.when(step < chunks)
    def _():
        for sub in range(CHUNK // 8):
            for part in range(parts):
                a = slice(sub * 8, sub * 8 + 8)
                b = slice(part * lanes, part * lanes + lanes)
                offset = SMAX - s_ref[a, b]
                which = k_ref[a, b]
                bits = [(offset & bit) != 0 for bit in (8, 4, 2, 1)]
                weights = [
                    jnp.take_along_axis(tab_ref[k], which, axis=1, mode="promise_in_bounds")
                    for k in range(taps)
                ]
                for c in range(2):
                    line = [prev_ref[g, c, i, a, b] for g in range(rows // GROUP) for i in range(GROUP)]
                    line += [own_ref[g, c, i, a, b] for g in range(rows // GROUP) for i in range(GROUP)]
                    line += [next_ref[0, c, i, a, b] for i in range(GROUP)]
                    line = [v.astype(f32) for v in line]
                    need = rows + taps - 1
                    for n, bit in enumerate((8, 4, 2, 1)):
                        keep = need + (bit - 1)
                        line = [
                            jnp.where(bits[n], line[j + bit], line[j]) if j + bit < len(line) else line[j]
                            for j in range(keep)
                        ]
                    for i in range(rows):
                        total = weights[0] * line[i + taps - 1]
                        for k in range(1, taps):
                            total = total + weights[k] * line[i + taps - 1 - k]
                        m_ref[i, a, c * inner + part * lanes : c * inner + part * lanes + lanes] = total
        flat = m_ref[...].reshape(rows * CHUNK, 2 * inner).astype(bf16)
        z = dot(flat, v2_ref[...]).reshape(rows, CHUNK, 2 * inner)
        re, im = z[:, :, :inner], z[:, :, inner:]
        tc, ts = t_ref[0][None], t_ref[1][None]
        first = pl.multiple_of(step * CHUNK, CHUNK)
        y_ref[:, 0, pl.ds(first, CHUNK), :] = (re * tc - im * ts).astype(bf16)
        y_ref[:, 1, pl.ds(first, CHUNK), :] = (re * ts + im * tc).astype(bf16)

    @pl.when(step >= chunks)
    def _():
        base = (step - chunks) * GROUP
        scale = 1.0 / math.sqrt(outer * inner)
        for r in range(GROUP):
            z = dot(v1_ref[...], y_ref[base + r].reshape(2 * outer, inner)) * scale
            for c in range(2):
                for h in range(parts):
                    o_ref[c, 0, pl.ds(h * GROUP + r, outer, stride=stride), :] = z[
                        c * outer : (c + 1) * outer, h * lanes : (h + 1) * lanes
                    ]


def per_device(echoes, doppler_filter, migration_shift, kernel_index, kernel_taps):
    rows = echoes.shape[1]
    pulses = echoes.shape[2]
    inner = F2
    outer = pulses // inner
    taps = kernel_taps.shape[1]
    groups = rows // GROUP
    tiles = pulses // 128
    count = lax.axis_size("rng")
    whole = lambda *shape: pl.BlockSpec(shape, lambda i: (0,) * len(shape))

    def order(table):
        return jnp.swapaxes(table.reshape(table.shape[:-1] + (inner, outer)), -1, -2)

    oc, osn = dft(outer)
    ic, isn = dft(inner)
    w1h, w1l = split(np.block([[oc, osn], [-osn, oc]]))
    w2h, w2l = split(np.block([[ic, -isn], [isn, ic]]))
    v2 = split(np.block([[ic, isn], [-isn, ic]]))[0]
    v1 = split(np.block([[oc, -osn], [osn, oc]]))[0]
    twist = twiddles(outer, inner)
    response = order(doppler_filter * (1.0 / math.sqrt(pulses)))
    signal = (
        echoes.reshape(2, groups, GROUP, tiles, 128)
        .transpose(0, 1, 3, 2, 4)
        .reshape(2, groups, tiles * GROUP, 128)
    )
    filtered = pl.pallas_call(
        functools.partial(forward_kernel, outer, inner),
        grid=(groups,),
        in_specs=[
            pl.BlockSpec((2, 1, tiles * GROUP, 128), lambda i: (0, i, 0, 0)),
            whole(*w1h.shape),
            whole(*w1h.shape),
            whole(*w2h.shape),
            whole(*w2h.shape),
            whole(*twist.shape),
            whole(*twist.shape),
        ],
        out_specs=pl.BlockSpec((1, 2, GROUP, outer, inner), lambda i: (i, 0, 0, 0, 0)),
        out_shape=jax.ShapeDtypeStruct((groups, 2, GROUP, outer, inner), bf16),
        scratch_shapes=[pltpu.VMEM((GROUP * outer, 2 * inner), bf16)] * 2,
        name="forward",
    )(signal, jnp.asarray(w1h), jnp.asarray(w1l), jnp.asarray(w2h), jnp.asarray(w2l), jnp.asarray(twist), response)
    shift = order(migration_shift)
    before, after = exchange(filtered, shift, count)
    table = jnp.broadcast_to(
        jnp.tile(kernel_taps.T, (1, 128 // kernel_taps.shape[0]))[:, None, :], (taps, 8, 128)
    )
    chunks = outer // CHUNK
    last = chunks - 1
    at = lambda i: jnp.minimum(i, last)
    image = pl.pallas_call(
        functools.partial(inverse_kernel, outer, inner, rows, taps, chunks),
        grid=(chunks + groups,),
        in_specs=[
            pl.BlockSpec((groups, 2, GROUP, CHUNK, inner), lambda i: (0, 0, 0, at(i), 0)),
            pl.BlockSpec((groups, 2, GROUP, CHUNK, inner), lambda i: (0, 0, 0, at(i), 0)),
            pl.BlockSpec((1, 2, GROUP, CHUNK, inner), lambda i: (0, 0, 0, at(i), 0)),
            pl.BlockSpec((CHUNK, inner), lambda i: (at(i), 0)),
            pl.BlockSpec((CHUNK, inner), lambda i: (at(i), 0)),
            whole(taps, 8, 128),
            pl.BlockSpec((2, CHUNK, inner), lambda i: (0, at(i), 0)),
            whole(*v2.shape),
            whole(*v1.shape),
        ],
        out_specs=pl.BlockSpec(
            (2, 1, tiles * GROUP, 128), lambda i: (0, jnp.maximum(i - chunks, 0), 0, 0)
        ),
        out_shape=jax.ShapeDtypeStruct((2, groups, tiles * GROUP, 128), f32),
        scratch_shapes=[
            pltpu.VMEM((rows, CHUNK, 2 * inner), f32),
            pltpu.VMEM((rows, 2, outer, inner), bf16),
        ],
        name="inverse",
    )(filtered, before, after, shift, order(kernel_index), table, jnp.asarray(twist), jnp.asarray(v2), jnp.asarray(v1))
    return (
        image.reshape(2, groups, tiles, GROUP, 128)
        .transpose(0, 1, 3, 2, 4)
        .reshape(2, rows, pulses)
    )


def solution(mesh):
    return jax.shard_map(
        per_device,
        mesh=mesh,
        in_specs=(P(None, ("swath", "rng"), None), P(), P(), P(), P()),
        out_specs=P(None, ("swath", "rng"), None),
        check_vma=False,
    )
```

```python
import functools
import math

import jax
import jax.numpy as jnp
import numpy as np
from jax import lax
from jax.experimental import pallas as pl
from jax.experimental.pallas import tpu as pltpu
from jax.sharding import PartitionSpec as P

F2 = 256
SMAX = 9
GROUP = 8
CHUNK = 16

f32 = jnp.float32
bf16 = jnp.bfloat16


def dft(length):
    numbers = np.arange(length)
    angles = (numbers[:, None] * numbers[None, :] % length) * (2.0 * math.pi / length)
    return np.cos(angles), np.sin(angles)


def split(table):
    table = table.astype(np.float32)
    high = table.astype(bf16)
    return high, (table - high.astype(np.float32)).astype(bf16)


def twiddles(outer, inner):
    angles = (np.arange(outer)[:, None] * np.arange(inner)[None, :]) * (
        2.0 * math.pi / (outer * inner)
    )
    return np.stack([np.cos(angles), np.sin(angles)]).astype(np.float32)


def dot(a, b):
    return jnp.dot(a, b, preferred_element_type=f32)


def halves(value):
    high = value.astype(bf16)
    return high, (value - high.astype(f32)).astype(bf16)


def forward_kernel(outer, inner, x_ref, w1h_ref, w1l_ref, w2h_ref, w2l_ref, t_ref, h_ref, s_ref, k_ref, o_ref, so_ref, ko_ref, rh_ref, rl_ref):
    lanes = 128
    parts = inner // lanes
    stride = GROUP * parts
    so_ref[...] = s_ref[...].T
    ko_ref[...] = k_ref[...].T
    norm = 1.0 / math.sqrt(outer * inner)
    hr, hi = h_ref[0].T * norm, h_ref[1].T * norm
    w1h = w1h_ref[...]
    w1l = w1l_ref[...]
    for r in range(GROUP):
        columns = []
        for c in range(2):
            columns.append(
                jnp.concatenate(
                    [
                        x_ref[c, 0, pl.ds(h * GROUP + r, outer, stride=stride), :]
                        for h in range(parts)
                    ],
                    axis=1,
                )
            )
        xh, xl = halves(jnp.concatenate(columns, axis=0))
        s = dot(w1h, xh) + dot(w1h, xl) + dot(w1l, xh)
        re, im = s[:outer], s[outer:]
        tc, ts = t_ref[0], t_ref[1]
        rows = pl.ds(r * outer, outer)
        a, b = halves(re * tc + im * ts)
        rh_ref[rows, :inner] = a
        rl_ref[rows, :inner] = b
        a, b = halves(im * tc - re * ts)
        rh_ref[rows, inner:] = a
        rl_ref[rows, inner:] = b
    per = 2
    for g in range(GROUP // per):
        rows = pl.ds(g * per * outer, per * outer)
        rh = rh_ref[rows, :]
        z = dot(rh, w2h_ref[...]) + dot(rh, w2l_ref[...]) + dot(rl_ref[rows, :], w2h_ref[...])
        for j in range(per):
            re = z[j * outer : (j + 1) * outer, :inner]
            im = z[j * outer : (j + 1) * outer, inner:]
            o_ref[0, 0, g * per + j] = (re * hr + im * hi).astype(bf16)
            o_ref[0, 1, g * per + j] = (im * hr - re * hi).astype(bf16)


def exchange_kernel(count, own, s_ref, prev, nxt, mid, low, head, mix, ssem, rsem, lsem):
    me = lax.axis_index("rng")
    role = me % 4
    first = me < 4
    final = me >= count - 4
    half = own.shape[3] // 2
    early, late = range(4), range(4, 8)

    def at(ref, p):
        group = (1 - p // 4) if ref.shape[0] == 2 else 0
        return ref.at[group, (p // 2) % 2, :, pl.ds((p % 2) * half, half), :]

    def copy(kind, p, src, dst, target):
        return pltpu.make_async_remote_copy(
            src_ref=at(src, p),
            dst_ref=at(dst, p),
            send_sem=ssem.at[kind, p],
            recv_sem=rsem.at[kind, p],
            device_id={"rng": target},
            device_id_type=pl.DeviceIdType.MESH,
        )

    def got(kind, p, dst):
        copy(kind, p, dst, dst, (me + 1) % count).wait_recv()

    def merge(p, high, lower):
        rows = pl.ds((p % 2) * half, half)
        limit = SMAX - s_ref[rows, :]
        for j in range(GROUP):
            where = (0, (p // 2) % 2, j, rows)
            mix[where] = jnp.where(
                limit <= j, high[where].astype(f32), lower[where].astype(f32)
            ).astype(bf16)

    def local(src, dst, slot):
        return pltpu.make_async_copy(src, dst, lsem.at[slot])

    @pl.when(role == 0)
    def _():
        sends = [copy(0, p, own, prev, me + 1) for p in range(8)]
        for s in sends:
            s.start()

        @pl.when(first)
        def _():
            low[...] = jnp.zeros_like(low)
            fills = [local(low.at[0], prev.at[g], g) for g in range(2)]
            for f in fills:
                f.start()
            for f in fills:
                f.wait()

        @pl.when(jnp.logical_not(first))
        def _():
            back = [copy(1, p, own, low, me - 3) for p in late]
            for s in back:
                s.start()
            for p in early:
                got(2, p, prev)
            for p in late:
                got(3, p, prev)
            for s in back:
                s.wait_send()

        for p in late:
            got(4, p, nxt)
        for s in sends:
            s.wait_send()

    @pl.when(role == 1)
    def _():
        sends = [copy(2, p, own, prev, me + 1) for p in early]
        sends += [copy(2, p, mix, prev, me + 1) for p in late]
        back = [copy(4, p, own, nxt, me - 1) for p in late]
        for p in early:
            sends[p].start()
        for s in back:
            s.start()
        fetch = local(own.at[0], head.at[0], 0)
        fetch.start()
        fetch.wait()

        @pl.when(final)
        def _():
            low[...] = jnp.zeros_like(low)

        def relay(p):
            got(2, p, mid)

            @pl.when(jnp.logical_not(final))
            def _():
                copy(3, p, mid, prev, me + 3).start()

        for p in late:
            relay(p)

            @pl.when(jnp.logical_not(final))
            def _():
                got(1, p, low)

            merge(p, head, low)
            sends[p].start()
        out = local(mid.at[0], nxt.at[0], 1)
        out.start()
        for p in range(8):
            got(0, p, prev)
        out.wait()
        for s in sends + back:
            s.wait_send()

        @pl.when(jnp.logical_not(final))
        def _():
            for p in late:
                copy(3, p, mid, prev, me + 3).wait_send()

    @pl.when(role == 2)
    def _():
        fetch = local(own.at[0], head.at[0], 0)
        fetch.start()
        sends = [copy(0, p, own, prev, me + 1) for p in range(8)]
        for s in sends:
            s.start()
        over = [copy(2, p, mix, mid, me - 1) for p in late]
        fetch.wait()
        for p in late:
            got(0, p, mid)
            merge(p, mid, head)
            over[p - 4].start()
        out = local(mid.at[0], nxt.at[0], 1)
        out.start()
        pass_on = [copy(3, p, prev, nxt, me + 1) for p in late]

        @pl.when(jnp.logical_not(first))
        def _():
            for p in early:
                got(3, p, mid)
                copy(2, p, mid, prev, me - 2).start()

        for p in early:
            got(2, p, prev)
        for p in late:
            got(2, p, prev)
            pass_on[p - 4].start()
        out.wait()
        for s in sends + over + pass_on:
            s.wait_send()

        @pl.when(jnp.logical_not(first))
        def _():
            for p in early:
                copy(2, p, mid, prev, me - 2).wait_send()

    @pl.when(role == 3)
    def _():
        sends = [copy(0, p, own, mid, me - 1) for p in late]
        for s in sends:
            s.start()

        @pl.when(jnp.logical_not(final))
        def _():
            for p in early:
                copy(3, p, own, mid, me + 3).start()

        for p in range(8):
            got(0, p, prev)
        for p in late:
            got(3, p, nxt)
        for s in sends:
            s.wait_send()

        @pl.when(jnp.logical_not(final))
        def _():
            for p in early:
                copy(3, p, own, mid, me + 3).wait_send()


def exchange(filtered, shift, count):
    if count % 4 or filtered.shape[0] != 2 or filtered.shape[2] != SMAX - 1:
        before = lax.ppermute(filtered, "rng", [(i, i + 1) for i in range(count - 1)])
        after = lax.ppermute(filtered[:1], "rng", [(i + 1, i) for i in range(count - 1)])
        return before, after
    short = (1,) + filtered.shape[1:]
    anywhere = pl.BlockSpec(memory_space=pl.ANY)
    return pl.pallas_call(
        functools.partial(exchange_kernel, count),
        in_specs=[anywhere, pl.BlockSpec(memory_space=pltpu.VMEM)],
        out_specs=[anywhere, anywhere],
        out_shape=[
            jax.ShapeDtypeStruct(filtered.shape, bf16),
            jax.ShapeDtypeStruct(short, bf16),
        ],
        scratch_shapes=[
            pltpu.VMEM(filtered.shape, bf16),
            pltpu.VMEM(short, bf16),
            pltpu.VMEM(short, bf16),
            pltpu.VMEM(short, bf16),
            pltpu.SemaphoreType.DMA((5, 8)),
            pltpu.SemaphoreType.DMA((5, 8)),
            pltpu.SemaphoreType.DMA((2,)),
        ],
        compiler_params=pltpu.CompilerParams(has_side_effects=True),
        name="exchange",
    )(filtered, shift)


def inverse_kernel(outer, inner, rows, taps, chunks, own_ref, prev_ref, next_ref, s_ref, k_ref, tab_ref, t_ref, v2_ref, v1_ref, o_ref, m_ref, y_ref):
    lanes = 128
    parts = inner // lanes
    stride = GROUP * parts
    step = pl.program_id(0)
    low = taps // 2 - 1

    @pl.when(step < chunks)
    def _():
        for sub in range(CHUNK // 8):
            for part in range(parts):
                a = slice(sub * 8, sub * 8 + 8)
                b = slice(part * lanes, part * lanes + lanes)
                offset = SMAX - s_ref[a, b]
                which = k_ref[a, b]
                bits = [(offset & bit) != 0 for bit in (8, 4, 2, 1)]
                weights = [
                    jnp.take_along_axis(tab_ref[k], which, axis=1, mode="promise_in_bounds")
                    for k in range(taps)
                ]
                for c in range(2):
                    line = [prev_ref[g, c, i, a, b] for g in range(rows // GROUP) for i in range(GROUP)]
                    line += [own_ref[g, c, i, a, b] for g in range(rows // GROUP) for i in range(GROUP)]
                    line += [next_ref[0, c, i, a, b] for i in range(GROUP)]
                    line = [v.astype(f32) for v in line]
                    need = rows + taps - 1
                    for n, bit in enumerate((8, 4, 2, 1)):
                        keep = need + (bit - 1)
                        line = [
                            jnp.where(bits[n], line[j + bit], line[j]) if j + bit < len(line) else line[j]
                            for j in range(keep)
                        ]
                    for i in range(rows):
                        total = weights[0] * line[i + taps - 1]
                        for k in range(1, taps):
                            total = total + weights[k] * line[i + taps - 1 - k]
                        m_ref[i, a, c * inner + part * lanes : c * inner + part * lanes + lanes] = total
        flat = m_ref[...].reshape(rows * CHUNK, 2 * inner).astype(bf16)
        z = dot(flat, v2_ref[...]).reshape(rows, CHUNK, 2 * inner)
        re, im = z[:, :, :inner], z[:, :, inner:]
        tc, ts = t_ref[0][None], t_ref[1][None]
        first = pl.multiple_of(step * CHUNK, CHUNK)
        y_ref[:, 0, pl.ds(first, CHUNK), :] = (re * tc - im * ts).astype(bf16)
        y_ref[:, 1, pl.ds(first, CHUNK), :] = (re * ts + im * tc).astype(bf16)

    @pl.when(step >= chunks)
    def _():
        base = (step - chunks) * GROUP
        scale = 1.0 / math.sqrt(outer * inner)
        for r in range(GROUP):
            z = dot(v1_ref[...], y_ref[base + r].reshape(2 * outer, inner)) * scale
            for c in range(2):
                for h in range(parts):
                    o_ref[c, 0, pl.ds(h * GROUP + r, outer, stride=stride), :] = z[
                        c * outer : (c + 1) * outer, h * lanes : (h + 1) * lanes
                    ]


def per_device(echoes, doppler_filter, migration_shift, kernel_index, kernel_taps):
    rows = echoes.shape[1]
    pulses = echoes.shape[2]
    inner = F2
    outer = pulses // inner
    taps = kernel_taps.shape[1]
    groups = rows // GROUP
    tiles = pulses // 128
    count = lax.axis_size("rng")
    whole = lambda *shape: pl.BlockSpec(shape, lambda i: (0,) * len(shape))

    oc, osn = dft(outer)
    ic, isn = dft(inner)
    w1h, w1l = split(np.block([[oc, osn], [-osn, oc]]))
    w2h, w2l = split(np.block([[ic, -isn], [isn, ic]]))
    v2 = split(np.block([[ic, isn], [-isn, ic]]))[0]
    v1 = split(np.block([[oc, -osn], [osn, oc]]))[0]
    twist = twiddles(outer, inner)
    signal = (
        echoes.reshape(2, groups, GROUP, tiles, 128)
        .transpose(0, 1, 3, 2, 4)
        .reshape(2, groups, tiles * GROUP, 128)
    )
    filtered, shift, which = pl.pallas_call(
        functools.partial(forward_kernel, outer, inner),
        grid=(groups,),
        in_specs=[
            pl.BlockSpec((2, 1, tiles * GROUP, 128), lambda i: (0, i, 0, 0)),
            whole(*w1h.shape),
            whole(*w1h.shape),
            whole(*w2h.shape),
            whole(*w2h.shape),
            whole(*twist.shape),
            whole(2, inner, outer),
            whole(inner, outer),
            whole(inner, outer),
        ],
        out_specs=[
            pl.BlockSpec((1, 2, GROUP, outer, inner), lambda i: (i, 0, 0, 0, 0)),
            whole(outer, inner),
            whole(outer, inner),
        ],
        out_shape=[
            jax.ShapeDtypeStruct((groups, 2, GROUP, outer, inner), bf16),
            jax.ShapeDtypeStruct((outer, inner), jnp.int32),
            jax.ShapeDtypeStruct((outer, inner), jnp.int32),
        ],
        scratch_shapes=[pltpu.VMEM((GROUP * outer, 2 * inner), bf16)] * 2,
        name="forward",
    )(signal, jnp.asarray(w1h), jnp.asarray(w1l), jnp.asarray(w2h), jnp.asarray(w2l), jnp.asarray(twist), doppler_filter.reshape(2, inner, outer), migration_shift.reshape(inner, outer), kernel_index.reshape(inner, outer))
    before, after = exchange(filtered, shift, count)
    table = jnp.broadcast_to(
        jnp.tile(kernel_taps.T, (1, 128 // kernel_taps.shape[0]))[:, None, :], (taps, 8, 128)
    )
    chunks = outer // CHUNK
    last = chunks - 1
    at = lambda i: jnp.minimum(i, last)
    image = pl.pallas_call(
        functools.partial(inverse_kernel, outer, inner, rows, taps, chunks),
        grid=(chunks + groups,),
        in_specs=[
            pl.BlockSpec((groups, 2, GROUP, CHUNK, inner), lambda i: (0, 0, 0, at(i), 0)),
            pl.BlockSpec((groups, 2, GROUP, CHUNK, inner), lambda i: (0, 0, 0, at(i), 0)),
            pl.BlockSpec((1, 2, GROUP, CHUNK, inner), lambda i: (0, 0, 0, at(i), 0)),
            pl.BlockSpec((CHUNK, inner), lambda i: (at(i), 0)),
            pl.BlockSpec((CHUNK, inner), lambda i: (at(i), 0)),
            whole(taps, 8, 128),
            pl.BlockSpec((2, CHUNK, inner), lambda i: (0, at(i), 0)),
            whole(*v2.shape),
            whole(*v1.shape),
        ],
        out_specs=pl.BlockSpec(
            (2, 1, tiles * GROUP, 128), lambda i: (0, jnp.maximum(i - chunks, 0), 0, 0)
        ),
        out_shape=jax.ShapeDtypeStruct((2, groups, tiles * GROUP, 128), f32),
        scratch_shapes=[
            pltpu.VMEM((rows, CHUNK, 2 * inner), f32),
            pltpu.VMEM((rows, 2, outer, inner), bf16),
        ],
        name="inverse",
    )(filtered, before, after, shift, which, table, jnp.asarray(twist), jnp.asarray(v2), jnp.asarray(v1))
    return (
        image.reshape(2, groups, tiles, GROUP, 128)
        .transpose(0, 1, 3, 2, 4)
        .reshape(2, rows, pulses)
    )


def solution(mesh):
    return jax.shard_map(
        per_device,
        mesh=mesh,
        in_specs=(P(None, ("swath", "rng"), None), P(), P(), P(), P()),
        out_specs=P(None, ("swath", "rng"), None),
        check_vma=False,
    )
```

```python
import functools
import math

import jax
import jax.numpy as jnp
import numpy as np
from jax import lax
from jax.experimental import pallas as pl
from jax.experimental.pallas import tpu as pltpu
from jax.sharding import PartitionSpec as P

F2 = 256
SMAX = 9
GROUP = 8
CHUNK = 16

f32 = jnp.float32
bf16 = jnp.bfloat16


def dft(length):
    numbers = np.arange(length)
    angles = (numbers[:, None] * numbers[None, :] % length) * (2.0 * math.pi / length)
    return np.cos(angles), np.sin(angles)


def split(table):
    table = table.astype(np.float32)
    high = table.astype(bf16)
    return high, (table - high.astype(np.float32)).astype(bf16)


def twiddles(outer, inner):
    angles = (np.arange(outer)[:, None] * np.arange(inner)[None, :]) * (
        2.0 * math.pi / (outer * inner)
    )
    return np.stack([np.cos(angles), np.sin(angles)]).astype(np.float32)


def dot(a, b):
    return jnp.dot(a, b, preferred_element_type=f32)


def halves(value):
    high = value.astype(bf16)
    return high, (value - high.astype(f32)).astype(bf16)


def forward_kernel(outer, inner, x_ref, w1h_ref, w1l_ref, w2h_ref, w2l_ref, t_ref, h_ref, s_ref, k_ref, o_ref, so_ref, ko_ref, rh_ref, rl_ref):
    lanes = 128
    parts = inner // lanes
    stride = GROUP * parts
    so_ref[...] = s_ref[...].T
    ko_ref[...] = k_ref[...].T
    norm = 1.0 / math.sqrt(outer * inner)
    hr, hi = h_ref[0].T * norm, h_ref[1].T * norm
    w1h = w1h_ref[...]
    w1l = w1l_ref[...]
    for r in range(GROUP):
        columns = []
        for c in range(2):
            columns.append(
                jnp.concatenate(
                    [
                        x_ref[c, 0, pl.ds(h * GROUP + r, outer, stride=stride), :]
                        for h in range(parts)
                    ],
                    axis=1,
                )
            )
        xh, xl = halves(jnp.concatenate(columns, axis=0))
        s = dot(w1h, xh) + dot(w1h, xl) + dot(w1l, xh)
        re, im = s[:outer], s[outer:]
        tc, ts = t_ref[0], t_ref[1]
        rows = pl.ds(r * outer, outer)
        a, b = halves(re * tc + im * ts)
        rh_ref[rows, :inner] = a
        rl_ref[rows, :inner] = b
        a, b = halves(im * tc - re * ts)
        rh_ref[rows, inner:] = a
        rl_ref[rows, inner:] = b
    per = 2
    for g in range(GROUP // per):
        rows = pl.ds(g * per * outer, per * outer)
        rh = rh_ref[rows, :]
        z = dot(rh, w2h_ref[...]) + dot(rh, w2l_ref[...]) + dot(rl_ref[rows, :], w2h_ref[...])
        for j in range(per):
            re = z[j * outer : (j + 1) * outer, :inner]
            im = z[j * outer : (j + 1) * outer, inner:]
            o_ref[0, 0, g * per + j] = (re * hr + im * hi).astype(bf16)
            o_ref[0, 1, g * per + j] = (im * hr - re * hi).astype(bf16)


def exchange_kernel(count, own, s_ref, prev, nxt, mid, low, head, mix, ssem, rsem, lsem):
    me = lax.axis_index("rng")
    role = me % 4
    first = me < 4
    final = me >= count - 4
    half = own.shape[3] // 2
    early, late = range(4), range(4, 8)

    def at(ref, p):
        group = (1 - p // 4) if ref.shape[0] == 2 else 0
        return ref.at[group, (p // 2) % 2, :, pl.ds((p % 2) * half, half), :]

    def copy(kind, p, src, dst, target):
        return pltpu.make_async_remote_copy(
            src_ref=at(src, p),
            dst_ref=at(dst, p),
            send_sem=ssem.at[kind, p],
            recv_sem=rsem.at[kind, p],
            device_id={"rng": target},
            device_id_type=pl.DeviceIdType.MESH,
        )

    def got(kind, p, dst):
        copy(kind, p, dst, dst, (me + 1) % count).wait_recv()

    def merge(p, high, lower):
        rows = pl.ds((p % 2) * half, half)
        limit = SMAX - s_ref[rows, :]
        for j in range(GROUP):
            where = (0, (p // 2) % 2, j, rows)
            mix[where] = jnp.where(
                limit <= j, high[where].astype(f32), lower[where].astype(f32)
            ).astype(bf16)

    def local(src, dst, slot):
        return pltpu.make_async_copy(src, dst, lsem.at[slot])

    @pl.when(role == 0)
    def _():
        sends = [copy(0, p, own, prev, me + 1) for p in range(8)]
        for s in sends:
            s.start()

        @pl.when(first)
        def _():
            low[...] = jnp.zeros_like(low)
            fills = [local(low.at[0], prev.at[g], g) for g in range(2)]
            for f in fills:
                f.start()
            for f in fills:
                f.wait()

        @pl.when(jnp.logical_not(first))
        def _():
            back = [copy(1, p, own, low, me - 3) for p in late]
            for s in back:
                s.start()
            for p in early:
                got(2, p, prev)
            for p in late:
                got(3, p, prev)
            for s in back:
                s.wait_send()

        for p in late:
            got(4, p, nxt)
        for s in sends:
            s.wait_send()

    @pl.when(role == 1)
    def _():
        sends = [copy(2, p, own, prev, me + 1) for p in early]
        sends += [copy(2, p, mix, prev, me + 1) for p in late]
        back = [copy(4, p, own, nxt, me - 1) for p in late]
        for p in early:
            sends[p].start()
        for s in back:
            s.start()
        fetch = local(own.at[0], head.at[0], 0)
        fetch.start()
        fetch.wait()

        @pl.when(final)
        def _():
            low[...] = jnp.zeros_like(low)

        def relay(p):
            got(2, p, mid)

            @pl.when(jnp.logical_not(final))
            def _():
                copy(3, p, mid, prev, me + 3).start()

        for p in late:
            relay(p)

            @pl.when(jnp.logical_not(final))
            def _():
                got(1, p, low)

            merge(p, head, low)
            sends[p].start()
        out = local(mid.at[0], nxt.at[0], 1)
        out.start()
        for p in range(8):
            got(0, p, prev)
        out.wait()
        for s in sends + back:
            s.wait_send()

        @pl.when(jnp.logical_not(final))
        def _():
            for p in late:
                copy(3, p, mid, prev, me + 3).wait_send()

    @pl.when(role == 2)
    def _():
        fetch = local(own.at[0], head.at[0], 0)
        fetch.start()
        sends = [copy(0, p, own, prev, me + 1) for p in range(8)]
        for s in sends:
            s.start()
        over = [copy(2, p, mix, mid, me - 1) for p in late]
        fetch.wait()
        for p in late:
            got(0, p, mid)
            merge(p, mid, head)
            over[p - 4].start()
        out = local(mid.at[0], nxt.at[0], 1)
        out.start()
        pass_on = [copy(3, p, prev, nxt, me + 1) for p in late]

        @pl.when(jnp.logical_not(first))
        def _():
            for p in early:
                got(3, p, mid)
                copy(2, p, mid, prev, me - 2).start()

        for p in early:
            got(2, p, prev)
        for p in late:
            got(2, p, prev)
            pass_on[p - 4].start()
        out.wait()
        for s in sends + over + pass_on:
            s.wait_send()

        @pl.when(jnp.logical_not(first))
        def _():
            for p in early:
                copy(2, p, mid, prev, me - 2).wait_send()

    @pl.when(role == 3)
    def _():
        sends = [copy(0, p, own, mid, me - 1) for p in late]
        for s in sends:
            s.start()

        @pl.when(jnp.logical_not(final))
        def _():
            for p in early:
                copy(3, p, own, mid, me + 3).start()

        for p in range(8):
            got(0, p, prev)
        for p in late:
            got(3, p, nxt)
        for s in sends:
            s.wait_send()

        @pl.when(jnp.logical_not(final))
        def _():
            for p in early:
                copy(3, p, own, mid, me + 3).wait_send()


def exchange(filtered, shift, count):
    if count % 4 or filtered.shape[0] != 2 or filtered.shape[2] != SMAX - 1:
        before = lax.ppermute(filtered, "rng", [(i, i + 1) for i in range(count - 1)])
        after = lax.ppermute(filtered[:1], "rng", [(i + 1, i) for i in range(count - 1)])
        return before, after
    short = (1,) + filtered.shape[1:]
    anywhere = pl.BlockSpec(memory_space=pl.ANY)
    return pl.pallas_call(
        functools.partial(exchange_kernel, count),
        in_specs=[anywhere, pl.BlockSpec(memory_space=pltpu.VMEM)],
        out_specs=[anywhere, anywhere],
        out_shape=[
            jax.ShapeDtypeStruct(filtered.shape, bf16),
            jax.ShapeDtypeStruct(short, bf16),
        ],
        scratch_shapes=[
            pltpu.VMEM(filtered.shape, bf16),
            pltpu.VMEM(short, bf16),
            pltpu.VMEM(short, bf16),
            pltpu.VMEM(short, bf16),
            pltpu.SemaphoreType.DMA((5, 8)),
            pltpu.SemaphoreType.DMA((5, 8)),
            pltpu.SemaphoreType.DMA((2,)),
        ],
        compiler_params=pltpu.CompilerParams(has_side_effects=True),
        name="exchange",
    )(filtered, shift)


def inverse_kernel(outer, inner, rows, taps, chunks, own_ref, prev_ref, next_ref, s_ref, k_ref, tab_ref, t_ref, v2_ref, v1_ref, o_ref, m_ref, y_ref):
    lanes = 128
    parts = inner // lanes
    stride = GROUP * parts
    step = pl.program_id(0)
    low = taps // 2 - 1

    @pl.when(step < chunks)
    def _():
        for sub in range(CHUNK // 8):
            for part in range(parts):
                a = slice(sub * 8, sub * 8 + 8)
                b = slice(part * lanes, part * lanes + lanes)
                offset = SMAX - s_ref[a, b]
                which = k_ref[a, b]
                bits = [(offset & bit) != 0 for bit in (8, 4, 2, 1)]
                weights = [
                    jnp.take_along_axis(jnp.broadcast_to(tab_ref[k : k + 1, :], (8, 128)), which, axis=1, mode="promise_in_bounds")
                    for k in range(taps)
                ]
                for c in range(2):
                    line = [prev_ref[g, c, i, a, b] for g in range(rows // GROUP) for i in range(GROUP)]
                    line += [own_ref[g, c, i, a, b] for g in range(rows // GROUP) for i in range(GROUP)]
                    line += [next_ref[0, c, i, a, b] for i in range(GROUP)]
                    line = [v.astype(f32) for v in line]
                    need = rows + taps - 1
                    for n, bit in enumerate((8, 4, 2, 1)):
                        keep = need + (bit - 1)
                        line = [
                            jnp.where(bits[n], line[j + bit], line[j]) if j + bit < len(line) else line[j]
                            for j in range(keep)
                        ]
                    for i in range(rows):
                        total = weights[0] * line[i + taps - 1]
                        for k in range(1, taps):
                            total = total + weights[k] * line[i + taps - 1 - k]
                        m_ref[i, a, c * inner + part * lanes : c * inner + part * lanes + lanes] = total
        flat = m_ref[...].reshape(rows * CHUNK, 2 * inner).astype(bf16)
        z = dot(flat, v2_ref[...]).reshape(rows, CHUNK, 2 * inner)
        re, im = z[:, :, :inner], z[:, :, inner:]
        tc, ts = t_ref[0][None], t_ref[1][None]
        first = pl.multiple_of(step * CHUNK, CHUNK)
        y_ref[:, 0, pl.ds(first, CHUNK), :] = (re * tc - im * ts).astype(bf16)
        y_ref[:, 1, pl.ds(first, CHUNK), :] = (re * ts + im * tc).astype(bf16)

    @pl.when(step >= chunks)
    def _():
        base = (step - chunks) * GROUP
        scale = 1.0 / math.sqrt(outer * inner)
        for r in range(GROUP):
            z = dot(v1_ref[...], y_ref[base + r].reshape(2 * outer, inner)) * scale
            for c in range(2):
                for h in range(parts):
                    o_ref[c, 0, pl.ds(h * GROUP + r, outer, stride=stride), :] = z[
                        c * outer : (c + 1) * outer, h * lanes : (h + 1) * lanes
                    ]


def per_device(echoes, doppler_filter, migration_shift, kernel_index, kernel_taps):
    rows = echoes.shape[1]
    pulses = echoes.shape[2]
    inner = F2
    outer = pulses // inner
    taps = kernel_taps.shape[1]
    groups = rows // GROUP
    tiles = pulses // 128
    count = lax.axis_size("rng")
    whole = lambda *shape: pl.BlockSpec(shape, lambda i: (0,) * len(shape))

    oc, osn = dft(outer)
    ic, isn = dft(inner)
    w1h, w1l = split(np.block([[oc, osn], [-osn, oc]]))
    w2h, w2l = split(np.block([[ic, -isn], [isn, ic]]))
    v2 = split(np.block([[ic, isn], [-isn, ic]]))[0]
    v1 = split(np.block([[oc, -osn], [osn, oc]]))[0]
    twist = twiddles(outer, inner)
    signal = (
        echoes.reshape(2, groups, GROUP, tiles, 128)
        .transpose(0, 1, 3, 2, 4)
        .reshape(2, groups, tiles * GROUP, 128)
    )
    filtered, shift, which = pl.pallas_call(
        functools.partial(forward_kernel, outer, inner),
        grid=(groups,),
        in_specs=[
            pl.BlockSpec((2, 1, tiles * GROUP, 128), lambda i: (0, i, 0, 0)),
            whole(*w1h.shape),
            whole(*w1h.shape),
            whole(*w2h.shape),
            whole(*w2h.shape),
            whole(*twist.shape),
            whole(2, inner, outer),
            whole(inner, outer),
            whole(inner, outer),
        ],
        out_specs=[
            pl.BlockSpec((1, 2, GROUP, outer, inner), lambda i: (i, 0, 0, 0, 0)),
            whole(outer, inner),
            whole(outer, inner),
        ],
        out_shape=[
            jax.ShapeDtypeStruct((groups, 2, GROUP, outer, inner), bf16),
            jax.ShapeDtypeStruct((outer, inner), jnp.int32),
            jax.ShapeDtypeStruct((outer, inner), jnp.int32),
        ],
        scratch_shapes=[pltpu.VMEM((GROUP * outer, 2 * inner), bf16)] * 2,
        name="forward",
    )(signal, jnp.asarray(w1h), jnp.asarray(w1l), jnp.asarray(w2h), jnp.asarray(w2l), jnp.asarray(twist), doppler_filter.reshape(2, inner, outer), migration_shift.reshape(inner, outer), kernel_index.reshape(inner, outer))
    before, after = exchange(filtered, shift, count)
    table = jnp.pad(kernel_taps.T, ((0, 0), (0, 128 - kernel_taps.shape[0])))
    chunks = outer // CHUNK
    last = chunks - 1
    at = lambda i: jnp.minimum(i, last)
    image = pl.pallas_call(
        functools.partial(inverse_kernel, outer, inner, rows, taps, chunks),
        grid=(chunks + groups,),
        in_specs=[
            pl.BlockSpec((groups, 2, GROUP, CHUNK, inner), lambda i: (0, 0, 0, at(i), 0)),
            pl.BlockSpec((groups, 2, GROUP, CHUNK, inner), lambda i: (0, 0, 0, at(i), 0)),
            pl.BlockSpec((1, 2, GROUP, CHUNK, inner), lambda i: (0, 0, 0, at(i), 0)),
            pl.BlockSpec((CHUNK, inner), lambda i: (at(i), 0)),
            pl.BlockSpec((CHUNK, inner), lambda i: (at(i), 0)),
            whole(taps, 128),
            pl.BlockSpec((2, CHUNK, inner), lambda i: (0, at(i), 0)),
            whole(*v2.shape),
            whole(*v1.shape),
        ],
        out_specs=pl.BlockSpec(
            (2, 1, tiles * GROUP, 128), lambda i: (0, jnp.maximum(i - chunks, 0), 0, 0)
        ),
        out_shape=jax.ShapeDtypeStruct((2, groups, tiles * GROUP, 128), f32),
        scratch_shapes=[
            pltpu.VMEM((rows, CHUNK, 2 * inner), f32),
            pltpu.VMEM((rows, 2, outer, inner), bf16),
        ],
        name="inverse",
    )(filtered, before, after, shift, which, table, jnp.asarray(twist), jnp.asarray(v2), jnp.asarray(v1))
    return (
        image.reshape(2, groups, tiles, GROUP, 128)
        .transpose(0, 1, 3, 2, 4)
        .reshape(2, rows, pulses)
    )


def solution(mesh):
    return jax.shard_map(
        per_device,
        mesh=mesh,
        in_specs=(P(None, ("swath", "rng"), None), P(), P(), P(), P()),
        out_specs=P(None, ("swath", "rng"), None),
        check_vma=False,
    )
```
